32 devices in a mesh: replica: 8 (over z, core), fsdp: 4 (over y, x).
Axes of the slice: x: 2, y: 2, z: 4, core: 2. Of those that a mesh axis runs over, the one named last changes fastest.
Arguments:
- acts: bfloat16 [1, 4096, 8192], P(None, ('replica', 'fsdp')), may hold values from -6 to 6
- key_cot: bfloat16 [1, 4096, 512], P(None, ('replica', 'fsdp')), may hold values from -0.29882812 to 0.29882812
- params: float32 [8192, 512], P('fsdp'), may hold values from -4 to 4
- moment_one: float32 [8192, 512], P('fsdp'), may hold values from -1.8 to 1.8
- moment_two: float32 [8192, 512], P('fsdp'), may hold values from 0.05 to 2
- outer_mom: float32 [8192, 512], P(('fsdp', 'replica')), may hold values from -1.8 to 1.8
Outputs:
- new_params: float32 [8192, 512], P(('fsdp', 'replica'))
- new_mom: float32 [8192, 512], P(('fsdp', 'replica'))
The draws below stay inside these ranges and needn't reach their ends.
All inputs are finite; a program needn't handle non-finite values.
Results may differ from the reference program's by a relative error of at most 0.0007.
Values may be sent and summed in bfloat16 or wider, within the bound.
A program may use at most 64 MiB of HBM per device.

```python
import math
import jax
import jax.numpy as jnp
from jax import lax

D = 8192
KVW = 512
TOK_DEV = 128
MICRO = 1
TOKENS = 4096
N_REPLICA = 8
N_FSDP = 4


def strengthened(values, rng, source, target, blocks, factor):
    owner, partner = [(jnp.arange(values.shape[dim]) // (values.shape[dim] // blocks)).reshape([-1 if axis == dim else 1 for axis in range(values.ndim)]) for dim in (source, target)]
    chosen = jax.random.permutation(rng, blocks)[partner]
    strong = (owner == chosen) | (owner == (partner + blocks // 2) % blocks)
    return jnp.where(strong, factor * values, values)


def block_levels(rng, extent, shards, low, high):
    level = 1.0
    for axis_at, blocks in shards:
        heights = jax.random.uniform(jax.random.fold_in(jax.random.fold_in(rng, 6), axis_at), (blocks,), jnp.float32, low / len(shards), high / len(shards))
        level = level * jnp.repeat(jnp.exp(heights), extent[axis_at] // blocks).reshape((-1,) + (1,) * (len(extent) - 1 - axis_at))
    return level


def bell_draw(own_key, shape, spread, most, cuts=(), held_as=jnp.bfloat16):
    level = block_levels(own_key, shape, cuts, -0.22, 0.18) if cuts else 1.0
    values = jax.random.normal(own_key, shape, jnp.float32) * spread * level
    return jnp.minimum(jnp.maximum(values, -most), most).astype(held_as)


def bell_draw_with(stream_key, shape, spread, bound, shards, heavy, held_as=jnp.bfloat16):
    drawn = spread * jax.random.normal(stream_key, shape, jnp.float32)
    if shards:
        drawn = drawn * block_levels(stream_key, shape, shards, -0.22, 0.18)
    return jnp.clip(strengthened(drawn, jax.random.fold_in(stream_key, 3), *heavy), -bound, bound).astype(held_as)


def setup_inputs(seed: int = 0) -> dict:
    splits = jax.random.split(jax.random.key(seed), 7)
    return {
        "acts": bell_draw_with(splits[0], (MICRO, TOKENS, D), 1.0, 6.0, ((1, 32),), (1, 2, 32, 2.75)),
        "key_cot": bell_draw(splits[1], (MICRO, TOKENS, KVW), 0.05, 0.29882812, ((1, 32),)),
        "params": bell_draw(splits[2], (D, KVW), 1.0, 4.0, ((0, 4),), jnp.float32),
        "moment_one": bell_draw(splits[3], (D, KVW), 0.3, 1.8, ((0, 4),), jnp.float32),
        "moment_two": jnp.clip(jnp.exp(math.log(2.0) - 3.6888794 * jax.random.uniform(splits[4], (D, KVW), jnp.float32) ** block_levels(splits[4], (D, KVW), ((0, 4),), -0.2, 0.2)), 0.05, 2.0),
        "outer_mom": bell_draw(splits[5], (D, KVW), 0.3, 1.8, ((0, 32),), jnp.float32),
    }


beta_one = 0.9
beta_two = 0.95
epsilon = 1e-08
inner_rate = 0.3
decay_rate = 0.1
outer_rate = 0.7
momentum = 0.9

def adamw_step(weights, first, second, gradient):
    first = beta_one * first + (1.0 - beta_one) * gradient
    second = beta_two * second + (1.0 - beta_two) * gradient * gradient
    weights = weights - inner_rate * (first / (jnp.sqrt(second) + epsilon) + decay_rate * weights)
    return (weights, first, second)

def reference(acts, key_cot, params, moment_one, moment_two, outer_mom):
    group_rows = TOK_DEV * N_FSDP

    def one_worker(running, worker):
        start_row = (worker * group_rows).astype(jnp.int32)
        inputs = lax.dynamic_slice_in_dim(acts, start_row, group_rows, 1).astype(jnp.float32)
        cotangent = lax.dynamic_slice_in_dim(key_cot, start_row, group_rows, 1).astype(jnp.float32)
        gradients = jnp.einsum('mtd,mtk->mdk', inputs, cotangent)
        weights, first, second = (params, moment_one, moment_two)
        for number in range(MICRO):
            weights, first, second = adamw_step(weights, first, second, gradients[number])
        return (running + (params - weights), None)
    summed, _ = lax.scan(one_worker, jnp.zeros(params.shape, jnp.float32), jnp.arange(N_REPLICA, dtype=jnp.int32))
    drift_mean = summed / N_REPLICA
    new_mom = momentum * outer_mom + drift_mean
    new_params = params - outer_rate * (drift_mean + momentum * new_mom)
    return (new_params, new_mom)
```

```python
import functools

import jax
import jax.numpy as jnp
from jax import lax
from jax.experimental import pallas as pl
from jax.experimental.pallas import tpu as pltpu
from jax.sharding import PartitionSpec as P

beta_one = 0.9
beta_two = 0.95
epsilon = 1e-08
inner_rate = 0.3
decay_rate = 0.1
outer_rate = 0.7
momentum = 0.9

MESH = pl.DeviceIdType.MESH
UNIT = 128


def adamw_direction(first, second, gradient):
    first = beta_one * first + (1.0 - beta_one) * gradient
    second = beta_two * second + (1.0 - beta_two) * gradient * gradient
    return first / (jnp.sqrt(second) + epsilon)


def kernel(
    n_rep, n_fsdp,
    acts_ref, cot_ref, first_ref, second_ref, total_ref,
    acts_buf, cot_buf, first_buf, second_buf, pair_out, pair_in, far_out, far_in, own_sum,
    acts_send, acts_recv, cot_send, cot_recv, pair_send, pair_recv, far_send, far_recv, state_sem, local_sem,
):
    rep = lax.axis_index("replica")
    shard = lax.axis_index("fsdp")
    n_line = n_rep // 2
    line = rep // 2
    core = lax.rem(rep, 2)
    partner = line * 2 + (1 - core)
    rows = first_ref.shape[0]
    block = rows // n_rep
    order = sorted(range(n_line), key=lambda o: (-min(o, n_line - o), -o))

    def line_of(offset):
        return lax.rem(line + offset, n_line)

    steps = []
    for k, offset in enumerate(order):
        steps.append((k, 0, line_of(offset) * 2 + (1 - core)))
        steps.append((k, 1, line_of(offset) * 2 + core))

    def rows_of(j):
        return pl.ds(pl.multiple_of(j * block, block), block)

    local = [
        pltpu.make_async_copy(cot_ref, cot_buf.at[0], local_sem.at[0]),
        pltpu.make_async_copy(
            acts_ref.at[:, pl.ds(pl.multiple_of(shard * rows, rows), rows)], acts_buf.at[0], local_sem.at[1]
        ),
    ]
    barrier = pltpu.get_barrier_semaphore()
    peers = []
    for d in range(1, n_fsdp):
        peers.append((rep, lax.rem(shard + d, n_fsdp)))
    peers.append((partner, shard))
    for o in range(1, n_line):
        peers.append((line_of(o) * 2 + core, shard))
    for peer in peers:
        pl.semaphore_signal(barrier, inc=1, device_id=peer, device_id_type=MESH)
    for copy in local:
        copy.start()
    state = []
    for i, (k, h, j) in enumerate(steps):
        pair = (
            pltpu.make_async_copy(first_ref.at[rows_of(j)], first_buf.at[rows_of(j)], state_sem.at[i, 0]),
            pltpu.make_async_copy(second_ref.at[rows_of(j)], second_buf.at[rows_of(j)], state_sem.at[i, 1]),
        )
        state.append(pair)
    pl.semaphore_wait(barrier, len(peers))

    cots = []
    for d in range(1, n_fsdp):
        copy = pltpu.make_async_remote_copy(
            src_ref=cot_ref, dst_ref=cot_buf.at[d],
            send_sem=cot_send.at[d], recv_sem=cot_recv.at[d],
            device_id=(rep, lax.rem(shard + d, n_fsdp)), device_id_type=MESH,
        )
        copy.start()
        cots.append(copy)
    moves = []
    for i, (k, h, j) in enumerate(steps):
        group = []
        for d in range(1, n_fsdp):
            target = lax.rem(shard + d, n_fsdp)
            copy = pltpu.make_async_remote_copy(
                src_ref=acts_ref.at[:, pl.ds(pl.multiple_of(target * rows + j * block, block), block)],
                dst_ref=acts_buf.at[d, :, rows_of(j)],
                send_sem=acts_send.at[i, d], recv_sem=acts_recv.at[i, d],
                device_id=(rep, target), device_id_type=MESH,
            )
            copy.start()
            group.append(copy)
        moves.append(group)
        for copy in state[i]:
            copy.start()

    for copy in local:
        copy.wait()
    for copy in cots:
        copy.wait_recv()

    tokens = acts_buf.shape[0] * acts_buf.shape[1]
    width = cot_buf.shape[2]
    sends = []
    for i, (k, h, j) in enumerate(steps):
        last = k == n_line - 1
        for copy in moves[i]:
            copy.wait_recv()
        for copy in state[i]:
            copy.wait()
        if h == 1:
            pairing.wait_recv()

        def unit(s, _, j=j, k=k, h=h, last=last):
            at = pl.ds(pl.multiple_of(j * block + s * UNIT, UNIT), UNIT)
            here = pl.ds(pl.multiple_of(s * UNIT, UNIT), UNIT)
            inputs = acts_buf[:, :, at].reshape(tokens, UNIT)
            gradient = lax.dot_general(
                inputs, cot_buf[...].reshape(tokens, width), (((0,), (0,)), ((), ())),
                preferred_element_type=jnp.float32,
            )
            value = adamw_direction(first_buf[at, :], second_buf[at, :], gradient)
            if h == 0:
                pair_out[k, here, :] = value.astype(jnp.bfloat16)
            else:
                value = value + pair_in[k, here, :].astype(jnp.float32)
                if last:
                    own_sum[here, :] = value
                else:
                    far_out[k, here, :] = value.astype(jnp.bfloat16)
            return 0

        lax.fori_loop(0, block // UNIT, unit, 0)
        if h == 0:
            pairing = pltpu.make_async_remote_copy(
                src_ref=pair_out.at[k], dst_ref=pair_in.at[k],
                send_sem=pair_send.at[k], recv_sem=pair_recv.at[k],
                device_id=(partner, shard), device_id_type=MESH,
            )
            pairing.start()
            sends.append(pairing)
        elif not last:
            copy = pltpu.make_async_remote_copy(
                src_ref=far_out.at[k], dst_ref=far_in.at[k],
                send_sem=far_send.at[k], recv_sem=far_recv.at[k],
                device_id=(j, shard), device_id_type=MESH,
            )
            copy.start()
            sends.append(copy)
            moves.append([copy])
    for group in moves[len(steps):]:
        for copy in group:
            copy.wait_recv()

    def finish(s, _):
        here = pl.ds(pl.multiple_of(s * UNIT, UNIT), UNIT)
        value = own_sum[here, :]
        for k in range(n_line - 1):
            value = value + far_in[k, here, :].astype(jnp.float32)
        total_ref[here, :] = value
        return 0

    lax.fori_loop(0, block // UNIT, finish, 0)
    for copy in cots + sends:
        copy.wait_send()
    for group in moves[: len(steps)]:
        for copy in group:
            copy.wait_send()


def fused_sum(acts, cot, first, second, n_rep, n_fsdp):
    tokens, width = cot.shape
    rows = first.shape[0]
    block = rows // n_rep
    n_line = n_rep // 2
    far = max(n_line - 1, 1)
    return pl.pallas_call(
        functools.partial(kernel, n_rep, n_fsdp),
        out_shape=jax.ShapeDtypeStruct((block, width), jnp.float32),
        in_specs=[pl.BlockSpec(memory_space=pl.ANY)] * 4,
        out_specs=pl.BlockSpec(memory_space=pltpu.VMEM),
        scratch_shapes=[
            pltpu.VMEM((n_fsdp, tokens, rows), jnp.bfloat16),
            pltpu.VMEM((n_fsdp, tokens, width), jnp.bfloat16),
            pltpu.VMEM((rows, width), jnp.float32),
            pltpu.VMEM((rows, width), jnp.float32),
            pltpu.VMEM((n_line, block, width), jnp.bfloat16),
            pltpu.VMEM((n_line, block, width), jnp.bfloat16),
            pltpu.VMEM((far, block, width), jnp.bfloat16),
            pltpu.VMEM((far, block, width), jnp.bfloat16),
            pltpu.VMEM((block, width), jnp.float32),
            pltpu.SemaphoreType.DMA((n_rep, n_fsdp)),
            pltpu.SemaphoreType.DMA((n_rep, n_fsdp)),
            pltpu.SemaphoreType.DMA((n_fsdp,)),
            pltpu.SemaphoreType.DMA((n_fsdp,)),
            pltpu.SemaphoreType.DMA((n_line,)),
            pltpu.SemaphoreType.DMA((n_line,)),
            pltpu.SemaphoreType.DMA((far,)),
            pltpu.SemaphoreType.DMA((far,)),
            pltpu.SemaphoreType.DMA((n_rep, 2)),
            pltpu.SemaphoreType.DMA((2,)),
        ],
        compiler_params=pltpu.CompilerParams(collective_id=0, has_side_effects=True),
    )(acts, cot, first, second)


def plain_sum(acts, cot, first, second):
    inputs = lax.all_to_all(acts, "fsdp", split_axis=1, concat_axis=0, tiled=True)
    cots = lax.all_gather(cot, "fsdp", axis=0, tiled=True)
    gradient = lax.dot_general(
        inputs, cots, (((0,), (0,)), ((), ())), preferred_element_type=jnp.float32
    )
    return lax.psum_scatter(
        adamw_direction(first, second, gradient), "replica", scatter_dimension=0, tiled=True
    )


def per_device(n_rep, n_fsdp, acts, key_cot, params, moment_one, moment_two, outer_mom):
    block = params.shape[0] // n_rep
    acts, key_cot = acts[0], key_cot[0]
    if block % UNIT == 0 and n_rep % 2 == 0 and n_fsdp > 1:
        total = fused_sum(acts, key_cot, moment_one, moment_two, n_rep, n_fsdp)
    else:
        total = plain_sum(acts, key_cot, moment_one, moment_two)
    anchor = lax.dynamic_slice_in_dim(params, lax.axis_index("replica") * block, block, 0)
    drift_mean = inner_rate * (total / n_rep + decay_rate * anchor)
    new_mom = momentum * outer_mom + drift_mean
    new_params = anchor - outer_rate * (drift_mean + momentum * new_mom)
    return (new_params, new_mom)


def solution(mesh):
    return jax.shard_map(
        functools.partial(per_device, mesh.shape["replica"], mesh.shape["fsdp"]),
        mesh=mesh,
        in_specs=(
            P(None, ("replica", "fsdp"), None),
            P(None, ("replica", "fsdp"), None),
            P("fsdp", None),
            P("fsdp", None),
            P("fsdp", None),
            P(("fsdp", "replica"), None),
        ),
        out_specs=(P(("fsdp", "replica"), None), P(("fsdp", "replica"), None)),
        check_vma=False,
    )
```

```python
import functools

import jax
import jax.numpy as jnp
from jax import lax
from jax.experimental import pallas as pl
from jax.experimental.pallas import tpu as pltpu
from jax.sharding import PartitionSpec as P

beta_one = 0.9
beta_two = 0.95
epsilon = 1e-08
inner_rate = 0.3
decay_rate = 0.1
outer_rate = 0.7
momentum = 0.9

MESH = pl.DeviceIdType.MESH
UNIT = 128

def adamw_direction(first, second, gradient):
    first = beta_one * first + (1.0 - beta_one) * gradient
    second = beta_two * second + (1.0 - beta_two) * gradient * gradient
    return first / (jnp.sqrt(second) + epsilon)

def kernel(
    n_rep, splits,
    acts_ref, cot_ref, params_ref, first_ref, second_ref, outer_ref, new_params_ref, new_mom_ref,
    acts_buf, cot_buf, first_buf, second_buf, pair_out, pair_in, far_out, far_in, own_sum, anchor_buf, outer_buf,
    acts_send, acts_recv, cot_send, cot_recv, pair_send, pair_recv, far_send, far_recv, state_sem, local_sem,
):
    rep = lax.axis_index("replica")
    shard = lax.axis_index("fsdp")
    line, core = lax.div(rep, 2), lax.rem(rep, 2)
    row_at, col_at = lax.div(shard, 2), lax.rem(shard, 2)
    rows = first_ref.shape[0]
    block = rows // n_rep
    half = cot_ref.shape[0] // 2
    tokens = acts_buf.shape[0] * acts_buf.shape[1]
    width = cot_buf.shape[2]
    partner = line * 2 + (1 - core)
    shards = (shard, row_at * 2 + (1 - col_at), (1 - row_at) * 2 + col_at, (1 - row_at) * 2 + (1 - col_at))
    lines = (line, line + 1 - 2 * lax.rem(line, 2), lax.rem(line + 2, 4), 3 - line)
    outer = 1 - lax.rem(lax.div(line, 2) + lax.rem(line, 2), 2)
    is_outer = outer == 1
    n_line = len(lines)

    units = []
    for k in range(n_line):
        other = lines[n_line - 1 - k]
        size = block // splits[k]
        for h, owner in ((0, 1 - core), (1, core)):
            for part in range(splits[k]):
                units.append((k, part * size, size, h, other * 2 + owner))

    def span(start, size):
        return pl.ds(pl.multiple_of(start, size), size)

    def remote(source, target, send, recv, device):
        return pltpu.make_async_remote_copy(
            src_ref=source, dst_ref=target, send_sem=send, recv_sem=recv, device_id=device, device_id_type=MESH
        )

    local = [
        pltpu.make_async_copy(cot_ref, cot_buf.at[0], local_sem.at[0]),
        pltpu.make_async_copy(acts_ref.at[:, span(shard * rows, rows)], acts_buf.at[0], local_sem.at[1]),
    ]
    state = []
    for i, (k, start, size, h, j) in enumerate(units):
        at = span(j * block + start, size)
        state.append((
            pltpu.make_async_copy(first_ref.at[at], first_buf.at[at], state_sem.at[i, 0]),
            pltpu.make_async_copy(second_ref.at[at], second_buf.at[at], state_sem.at[i, 1]),
        ))
    barrier = pltpu.get_barrier_semaphore()
    peers = [(rep, shards[d]) for d in range(1, 4)] + [(partner, shard)]
    peers += [(lines[o] * 2 + core, shard) for o in (1, 2)]
    for peer in peers:
        pl.semaphore_signal(barrier, inc=1, device_id=peer, device_id_type=MESH)

    @pl.when(jnp.logical_not(is_outer))
    def _():
        pl.semaphore_signal(barrier, inc=1, device_id=(lines[3] * 2 + core, shard), device_id_type=MESH)

    for copy in local:
        copy.start()
    pl.semaphore_wait(barrier, len(peers) + 1 - outer)

    sends = []
    cots = []
    for d in (1, 2):
        copy = remote(cot_ref, cot_buf.at[d], cot_send.at[d], cot_recv.at[d], (rep, shards[d]))
        copy.start()
        cots.append(copy)
    moves = []

    def issue(i):
        k, start, size, h, j = units[i]
        group = []
        for d in (3, 1, 2):
            copy = remote(
                acts_ref.at[:, span(shards[d] * rows + j * block + start, size)],
                acts_buf.at[d, :, span(j * block + start, size)],
                acts_send.at[i, d], acts_recv.at[i, d], (rep, shards[d]),
            )
            copy.start()
            group.append(copy)
        moves.append(group)
        for copy in state[i]:
            copy.start()

    for i in range(2):
        issue(i)
    for d, via in ((1, 2), (2, 1)):
        cots[d - 1].wait_recv()
        piece = pl.ds((d - 1) * half, half)
        copy = remote(
            cot_buf.at[d, piece], cot_buf.at[3, piece], cot_send.at[d + 2], cot_recv.at[d + 2], (rep, shards[via])
        )
        copy.start()
        cots.append(copy)
    for i in range(2, len(units)):
        issue(i)
    finals = [
        pltpu.make_async_copy(params_ref.at[span(rep * block, block)], anchor_buf, local_sem.at[2]),
        pltpu.make_async_copy(outer_ref, outer_buf, local_sem.at[3]),
    ]
    for copy in finals:
        copy.start()
    for copy in local:
        copy.wait()
    for copy in cots[2:]:
        copy.wait_recv()

    far_sends = []
    pairings = {}
    for i, (k, start, size, h, j) in enumerate(units):
        last = k == n_line - 1
        for copy in moves[i]:
            copy.wait_recv()
        for copy in state[i]:
            copy.wait()
        at = span(j * block + start, size)
        here = pl.ds(start, size)
        gradient = lax.dot_general(
            acts_buf[:, :, at].reshape(tokens, size), cot_buf[...].reshape(tokens, width),
            (((0,), (0,)), ((), ())), preferred_element_type=jnp.float32,
        )
        value = adamw_direction(first_buf[at, :], second_buf[at, :], gradient)
        sem = (k, start // size)
        if h == 0:
            pair_out[k, here, :] = value
            pairing = remote(
                pair_out.at[k, here], pair_in.at[k, here], pair_send.at[sem], pair_recv.at[sem], (partner, shard)
            )
            pairing.start()
            pairings[sem] = pairing
            sends.append(pairing)
            continue
        pairings[sem].wait_recv()
        value = value + pair_in[k, here, :]
        if last:
            own_sum[here, :] = value
            continue
        if k == 0:
            slot = outer * 3
            device = ((outer * lines[1] + (1 - outer) * lines[3]) * 2 + core, shard)
        else:
            slot = k
            device = (j, shard)
        if k == 1:
            arrival = remote(
                far_out.at[k, here], far_in.at[3, here],
                far_send.at[3, start // size], far_recv.at[3, start // size], device,
            )

            @pl.when(is_outer)
            def _(value=value, k=k, here=here):
                far_out[k, here, :] = value.astype(jnp.bfloat16)

            @pl.when(jnp.logical_not(is_outer))
            def _(value=value, k=k, here=here, arrival=arrival):
                arrival.wait_recv()
                far_out[k, here, :] = (value + far_in[3, here, :].astype(jnp.float32)).astype(jnp.bfloat16)
        else:
            far_out[k, here, :] = value.astype(jnp.bfloat16)
        copy = remote(
            far_out.at[k, here], far_in.at[slot, here],
            far_send.at[sem], far_recv.at[slot, start // size], device,
        )
        copy.start()
        far_sends.append((k, start, size, copy))

    for k, start, size, copy in far_sends:
        if k > 0:
            copy.wait_recv()
        else:
            arrival = remote(
                far_out.at[0, pl.ds(start, size)], far_in.at[0, pl.ds(start, size)],
                far_send.at[0, start // size], far_recv.at[0, start // size], (rep, shard),
            )

            @pl.when(jnp.logical_not(is_outer))
            def _(arrival=arrival):
                arrival.wait_recv()

    @pl.when(jnp.logical_not(is_outer))
    def _():
        own_sum[...] = own_sum[...] + far_in[0].astype(jnp.float32)

    for copy in finals:
        copy.wait()
    anchor = anchor_buf[...]
    total = own_sum[...] + (far_in[1].astype(jnp.float32) + far_in[2].astype(jnp.float32))
    drift_mean = inner_rate * (total / n_rep + decay_rate * anchor)
    new_mom = momentum * outer_buf[...] + drift_mean
    new_params_ref[...] = anchor - outer_rate * (drift_mean + momentum * new_mom)
    new_mom_ref[...] = new_mom

    for copy in cots + sends + [entry[3] for entry in far_sends]:
        copy.wait_send()
    for group in moves:
        for copy in group:
            copy.wait_send()

def fused_round(acts, cot, params, first, second, outer, n_rep, n_fsdp):
    tokens, width = cot.shape
    rows = first.shape[0]
    block = rows // n_rep
    n_line = n_rep // 2
    splits = (block // UNIT,) * n_line
    units = 2 * sum(splits)
    parts = max(splits)
    return pl.pallas_call(
        functools.partial(kernel, n_rep, splits),
        out_shape=(pltpu.VMEM((block, width), jnp.float32),) * 2,
        in_specs=[pl.BlockSpec(memory_space=pltpu.HBM)] * 6,
        out_specs=(pl.BlockSpec(memory_space=pltpu.VMEM),) * 2,
        scratch_shapes=[
            pltpu.VMEM((n_fsdp, tokens, rows), jnp.bfloat16),
            pltpu.VMEM((n_fsdp, tokens, width), jnp.bfloat16),
            pltpu.VMEM((rows, width), jnp.float32),
            pltpu.VMEM((rows, width), jnp.float32),
            pltpu.VMEM((n_line, block, width), jnp.float32),
            pltpu.VMEM((n_line, block, width), jnp.float32),
            pltpu.VMEM((n_line, block, width), jnp.bfloat16),
            pltpu.VMEM((n_line, block, width), jnp.bfloat16),
            pltpu.VMEM((block, width), jnp.float32),
            pltpu.VMEM((block, width), jnp.float32),
            pltpu.VMEM((block, width), jnp.float32),
            pltpu.SemaphoreType.DMA((units, n_fsdp)),
            pltpu.SemaphoreType.DMA((units, n_fsdp)),
            pltpu.SemaphoreType.DMA((5,)),
            pltpu.SemaphoreType.DMA((5,)),
            pltpu.SemaphoreType.DMA((n_line, parts)),
            pltpu.SemaphoreType.DMA((n_line, parts)),
            pltpu.SemaphoreType.DMA((n_line, parts)),
            pltpu.SemaphoreType.DMA((n_line, parts)),
            pltpu.SemaphoreType.DMA((units, 2)),
            pltpu.SemaphoreType.DMA((4,)),
        ],
        compiler_params=pltpu.CompilerParams(collective_id=0, has_side_effects=True),
    )(acts, cot, params, first, second, outer)

def plain_sum(acts, cot, first, second):
    inputs = lax.all_to_all(acts, "fsdp", split_axis=1, concat_axis=0, tiled=True)
    cots = lax.all_gather(cot, "fsdp", axis=0, tiled=True)
    gradient = lax.dot_general(
        inputs, cots, (((0,), (0,)), ((), ())), preferred_element_type=jnp.float32
    )
    return lax.psum_scatter(
        adamw_direction(first, second, gradient), "replica", scatter_dimension=0, tiled=True
    )

def per_device(n_rep, n_fsdp, acts, key_cot, params, moment_one, moment_two, outer_mom):
    block = params.shape[0] // n_rep
    acts, key_cot = acts[0], key_cot[0]
    if block % UNIT == 0 and n_rep == 8 and n_fsdp == 4:
        return fused_round(acts, key_cot, params, moment_one, moment_two, outer_mom, n_rep, n_fsdp)
    total = plain_sum(acts, key_cot, moment_one, moment_two)
    anchor = lax.dynamic_slice_in_dim(params, lax.axis_index("replica") * block, block, 0)
    drift_mean = inner_rate * (total / n_rep + decay_rate * anchor)
    new_mom = momentum * outer_mom + drift_mean
    new_params = anchor - outer_rate * (drift_mean + momentum * new_mom)
    return (new_params, new_mom)

def solution(mesh):
    return jax.shard_map(
        functools.partial(per_device, mesh.shape["replica"], mesh.shape["fsdp"]),
        mesh=mesh,
        in_specs=(
            P(None, ("replica", "fsdp"), None),
            P(None, ("replica", "fsdp"), None),
            P("fsdp", None),
            P("fsdp", None),
            P("fsdp", None),
            P(("fsdp", "replica"), None),
        ),
        out_specs=(P(("fsdp", "replica"), None), P(("fsdp", "replica"), None)),
        check_vma=False,
    )
```

```python
import functools

import jax
import jax.numpy as jnp
from jax import lax
from jax.experimental import pallas as pl
from jax.experimental.pallas import tpu as pltpu
from jax.sharding import PartitionSpec as P

beta_one = 0.9
beta_two = 0.95
epsilon = 1e-08
inner_rate = 0.3
decay_rate = 0.1
outer_rate = 0.7
momentum = 0.9

MESH = pl.DeviceIdType.MESH
UNIT = 128
WINDOW = 4

def adamw_direction(first, second, gradient):
    first = beta_one * first + (1.0 - beta_one) * gradient
    second = beta_two * second + (1.0 - beta_two) * gradient * gradient
    return first / (jnp.sqrt(second) + epsilon)

def kernel(
    n_rep, splits,
    acts_ref, cot_ref, params_ref, first_ref, second_ref, outer_ref, new_params_ref, new_mom_ref,
    acts_buf, cot_buf, first_buf, second_buf, pair_out, pair_in, far_out, far_in, own_sum, anchor_buf, outer_buf,
    acts_send, acts_recv, cot_send, cot_recv, pair_send, pair_recv, far_send, far_recv, state_sem, local_sem,
):
    rep = lax.axis_index("replica")
    shard = lax.axis_index("fsdp")
    line, core = lax.div(rep, 2), lax.rem(rep, 2)
    row_at, col_at = lax.div(shard, 2), lax.rem(shard, 2)
    rows = first_ref.shape[0]
    block = rows // n_rep
    half = cot_ref.shape[0] // 2
    tokens = acts_buf.shape[0] * acts_buf.shape[1]
    width = cot_buf.shape[2]
    partner = line * 2 + (1 - core)
    shards = (shard, row_at * 2 + (1 - col_at), (1 - row_at) * 2 + col_at, (1 - row_at) * 2 + (1 - col_at))
    lines = (line, line + 1 - 2 * lax.rem(line, 2), lax.rem(line + 2, 4), 3 - line)
    outer = 1 - lax.rem(lax.div(line, 2) + lax.rem(line, 2), 2)
    is_outer = outer == 1
    n_line = len(lines)

    units = []
    for k in range(n_line):
        other = lines[n_line - 1 - k]
        size = block // splits[k]
        for h, owner in ((0, 1 - core), (1, core)):
            for part in range(splits[k]):
                units.append((k, part * size, size, h, other * 2 + owner))

    def span(start, size):
        return pl.ds(pl.multiple_of(start, size), size)

    def remote(source, target, send, recv, device):
        return pltpu.make_async_remote_copy(
            src_ref=source, dst_ref=target, send_sem=send, recv_sem=recv, device_id=device, device_id_type=MESH
        )

    local = [
        pltpu.make_async_copy(cot_ref, cot_buf.at[0], local_sem.at[0]),
        pltpu.make_async_copy(acts_ref.at[:, span(shard * rows, rows)], acts_buf.at[0], local_sem.at[1]),
    ]
    state = []
    for i, (k, start, size, h, j) in enumerate(units):
        at = span(j * block + start, size)
        state.append((
            pltpu.make_async_copy(first_ref.at[at], first_buf.at[at], state_sem.at[i, 0]),
            pltpu.make_async_copy(second_ref.at[at], second_buf.at[at], state_sem.at[i, 1]),
        ))
    barrier = pltpu.get_barrier_semaphore()
    peers = [(rep, shards[d]) for d in range(1, 4)] + [(partner, shard)]
    peers += [(lines[o] * 2 + core, shard) for o in (1, 2)]
    for peer in peers:
        pl.semaphore_signal(barrier, inc=1, device_id=peer, device_id_type=MESH)

    @pl.when(jnp.logical_not(is_outer))
    def _():
        pl.semaphore_signal(barrier, inc=1, device_id=(lines[3] * 2 + core, shard), device_id_type=MESH)

    for copy in local:
        copy.start()
    pl.semaphore_wait(barrier, len(peers) + 1 - outer)

    sends = []
    cots = []
    for d in (1, 2):
        copy = remote(cot_ref, cot_buf.at[d], cot_send.at[d], cot_recv.at[d], (rep, shards[d]))
        copy.start()
        cots.append(copy)
    moves = []

    def issue(i):
        k, start, size, h, j = units[i]
        group = []
        for d in (3, 1, 2):
            copy = remote(
                acts_ref.at[:, span(shards[d] * rows + j * block + start, size)],
                acts_buf.at[d, :, span(j * block + start, size)],
                acts_send.at[i, d], acts_recv.at[i, d], (rep, shards[d]),
            )
            copy.start()
            group.append(copy)
        moves.append(group)
        for copy in state[i]:
            copy.start()

    for i in range(2):
        issue(i)
    for d, via in ((1, 2), (2, 1)):
        cots[d - 1].wait_recv()
        piece = pl.ds((d - 1) * half, half)
        copy = remote(
            cot_buf.at[d, piece], cot_buf.at[3, piece], cot_send.at[d + 2], cot_recv.at[d + 2], (rep, shards[via])
        )
        copy.start()
        cots.append(copy)
    for i in range(2, WINDOW):
        issue(i)
    finals = [
        pltpu.make_async_copy(params_ref.at[span(rep * block, block)], anchor_buf, local_sem.at[2]),
        pltpu.make_async_copy(outer_ref, outer_buf, local_sem.at[3]),
    ]
    for copy in finals:
        copy.start()
    for copy in local:
        copy.wait()
    for copy in cots[2:]:
        copy.wait_recv()

    far_sends = []
    pairings = {}
    for i, (k, start, size, h, j) in enumerate(units):
        last = k == n_line - 1
        for copy in moves[i]:
            copy.wait_recv()
        if i + WINDOW < len(units):
            issue(i + WINDOW)
        for copy in state[i]:
            copy.wait()
        at = span(j * block + start, size)
        here = pl.ds(start, size)
        gradient = lax.dot_general(
            acts_buf[:, :, at].reshape(tokens, size), cot_buf[...].reshape(tokens, width),
            (((0,), (0,)), ((), ())), preferred_element_type=jnp.float32,
        )
        value = adamw_direction(first_buf[at, :], second_buf[at, :], gradient)
        sem = (k, start // size)
        if h == 0:
            pair_out[k, here, :] = value
            pairing = remote(
                pair_out.at[k, here], pair_in.at[k, here], pair_send.at[sem], pair_recv.at[sem], (partner, shard)
            )
            pairing.start()
            pairings[sem] = pairing
            sends.append(pairing)
            continue
        pairings[sem].wait_recv()
        value = value + pair_in[k, here, :]
        if last:
            own_sum[here, :] = value
            continue
        if k == 0:
            slot = outer * 3
            device = ((outer * lines[1] + (1 - outer) * lines[3]) * 2 + core, shard)
        else:
            slot = k
            device = (j, shard)
        if k == 1:
            arrival = remote(
                far_out.at[k, here], far_in.at[3, here],
                far_send.at[3, start // size], far_recv.at[3, start // size], device,
            )

            @pl.when(is_outer)
            def _(value=value, k=k, here=here):
                far_out[k, here, :] = value.astype(jnp.bfloat16)

            @pl.when(jnp.logical_not(is_outer))
            def _(value=value, k=k, here=here, arrival=arrival):
                arrival.wait_recv()
                far_out[k, here, :] = (value + far_in[3, here, :].astype(jnp.float32)).astype(jnp.bfloat16)
        else:
            far_out[k, here, :] = value.astype(jnp.bfloat16)
        copy = remote(
            far_out.at[k, here], far_in.at[slot, here],
            far_send.at[sem], far_recv.at[slot, start // size], device,
        )
        copy.start()
        far_sends.append((k, start, size, copy))

    for k, start, size, copy in far_sends:
        if k > 0:
            copy.wait_recv()
        else:
            arrival = remote(
                far_out.at[0, pl.ds(start, size)], far_in.at[0, pl.ds(start, size)],
                far_send.at[0, start // size], far_recv.at[0, start // size], (rep, shard),
            )

            @pl.when(jnp.logical_not(is_outer))
            def _(arrival=arrival):
                arrival.wait_recv()

    @pl.when(jnp.logical_not(is_outer))
    def _():
        own_sum[...] = own_sum[...] + far_in[0].astype(jnp.float32)

    for copy in finals:
        copy.wait()
    anchor = anchor_buf[...]
    total = own_sum[...] + (far_in[1].astype(jnp.float32) + far_in[2].astype(jnp.float32))
    drift_mean = inner_rate * (total / n_rep + decay_rate * anchor)
    new_mom = momentum * outer_buf[...] + drift_mean
    new_params_ref[...] = anchor - outer_rate * (drift_mean + momentum * new_mom)
    new_mom_ref[...] = new_mom

    for copy in cots + sends + [entry[3] for entry in far_sends]:
        copy.wait_send()
    for group in moves:
        for copy in group:
            copy.wait_send()

def fused_round(acts, cot, params, first, second, outer, n_rep, n_fsdp):
    tokens, width = cot.shape
    rows = first.shape[0]
    block = rows // n_rep
    n_line = n_rep // 2
    splits = (block // UNIT,) * n_line
    units = 2 * sum(splits)
    parts = max(splits)
    return pl.pallas_call(
        functools.partial(kernel, n_rep, splits),
        out_shape=(pltpu.VMEM((block, width), jnp.float32),) * 2,
        in_specs=[pl.BlockSpec(memory_space=pltpu.HBM)] * 6,
        out_specs=(pl.BlockSpec(memory_space=pltpu.VMEM),) * 2,
        scratch_shapes=[
            pltpu.VMEM((n_fsdp, tokens, rows), jnp.bfloat16),
            pltpu.VMEM((n_fsdp, tokens, width), jnp.bfloat16),
            pltpu.VMEM((rows, width), jnp.float32),
            pltpu.VMEM((rows, width), jnp.float32),
            pltpu.VMEM((n_line, block, width), jnp.float32),
            pltpu.VMEM((n_line, block, width), jnp.float32),
            pltpu.VMEM((n_line, block, width), jnp.bfloat16),
            pltpu.VMEM((n_line, block, width), jnp.bfloat16),
            pltpu.VMEM((block, width), jnp.float32),
            pltpu.VMEM((block, width), jnp.float32),
            pltpu.VMEM((block, width), jnp.float32),
            pltpu.SemaphoreType.DMA((units, n_fsdp)),
            pltpu.SemaphoreType.DMA((units, n_fsdp)),
            pltpu.SemaphoreType.DMA((5,)),
            pltpu.SemaphoreType.DMA((5,)),
            pltpu.SemaphoreType.DMA((n_line, parts)),
            pltpu.SemaphoreType.DMA((n_line, parts)),
            pltpu.SemaphoreType.DMA((n_line, parts)),
            pltpu.SemaphoreType.DMA((n_line, parts)),
            pltpu.SemaphoreType.DMA((units, 2)),
            pltpu.SemaphoreType.DMA((4,)),
        ],
        compiler_params=pltpu.CompilerParams(collective_id=0, has_side_effects=True),
    )(acts, cot, params, first, second, outer)

def plain_sum(acts, cot, first, second):
    inputs = lax.all_to_all(acts, "fsdp", split_axis=1, concat_axis=0, tiled=True)
    cots = lax.all_gather(cot, "fsdp", axis=0, tiled=True)
    gradient = lax.dot_general(
        inputs, cots, (((0,), (0,)), ((), ())), preferred_element_type=jnp.float32
    )
    return lax.psum_scatter(
        adamw_direction(first, second, gradient), "replica", scatter_dimension=0, tiled=True
    )

def per_device(n_rep, n_fsdp, acts, key_cot, params, moment_one, moment_two, outer_mom):
    block = params.shape[0] // n_rep
    acts, key_cot = acts[0], key_cot[0]
    if block % UNIT == 0 and n_rep == 8 and n_fsdp == 4:
        return fused_round(acts, key_cot, params, moment_one, moment_two, outer_mom, n_rep, n_fsdp)
    total = plain_sum(acts, key_cot, moment_one, moment_two)
    anchor = lax.dynamic_slice_in_dim(params, lax.axis_index("replica") * block, block, 0)
    drift_mean = inner_rate * (total / n_rep + decay_rate * anchor)
    new_mom = momentum * outer_mom + drift_mean
    new_params = anchor - outer_rate * (drift_mean + momentum * new_mom)
    return (new_params, new_mom)

def solution(mesh):
    return jax.shard_map(
        functools.partial(per_device, mesh.shape["replica"], mesh.shape["fsdp"]),
        mesh=mesh,
        in_specs=(
            P(None, ("replica", "fsdp"), None),
            P(None, ("replica", "fsdp"), None),
            P("fsdp", None),
            P("fsdp", None),
            P("fsdp", None),
            P(("fsdp", "replica"), None),
        ),
        out_specs=(P(("fsdp", "replica"), None), P(("fsdp", "replica"), None)),
        check_vma=False,
    )
```
